256 devices in a mesh: sec: 4 (over z_lo), row: 8 (over x, core), col: 8 (over y, z_hi).
Axes of the slice: x: 4, y: 4, z: 8 (z_hi: 2, z_lo: 4; z = z_hi * 4 + z_lo), core: 2. Of those that a mesh axis runs over, the one named last changes fastest.
Arguments:
- amps: bfloat16 [16, 32, 32, 512], P(None, ('sec', 'row'), 'col'), may hold values from -6 to 6
- driver: bfloat16 [16, 32, 32, 512], P(None, 'col', ('sec', 'row')), may hold values from -6 to 6
- ladder_operator: bfloat16 [16384, 16384], P('col', ('sec', 'row')), as said below
- ladder_block_mask: int32 [128, 128], P('col', ('sec', 'row')), may hold values from 0 to 1, as said below
- cycle_op: bfloat16 [16384, 16384], P(('sec', 'row'), 'col'), as said below
- cycle_mask: int32 [128, 128], P(('sec', 'row'), 'col'), may hold values from 0 to 1, as said below
- occ_i: float32 [16], replicated, may hold values from -2 to -0.3
- occ_j: float32 [32], replicated, may hold values from -2 to -0.3
- vir_a: float32 [32], replicated, may hold values from 0.2 to 3
- vir_b: float32 [512], replicated, may hold values from 0.2 to 3
Outputs:
- amp_one: float32 [16, 32, 32, 512], P(None, 'col', ('sec', 'row'))
- amp_two: float32 [16, 32, 32, 512], P(None, ('sec', 'row'), 'col')
The draws below stay inside these ranges and needn't reach their ends.
Inputs may be any that keep to these rules, and one draw needn't show every extreme that they name: ladder_operator is symmetric. cycle_op is symmetric. ladder_block_mask is symmetric with ones on its diagonal. cycle_mask is symmetric with ones on its diagonal.
All inputs are finite; a program needn't handle non-finite values.
Results may differ from the reference program's by a relative error of at most 0.0024.
Values may be sent and summed in bfloat16 or wider, within the bound.
No kernel may reach another device: no remote copies, remote signals or barrier semaphores. Data moves between devices by JAX's collectives and lax.ppermute only.
A program may use at most 64 MiB of HBM per device.

```python
import jax
import jax.numpy as jnp

OCCUPIED_FIRST = 16
OCCUPIED_SECOND = 32
VIRTUAL_SLAB = 32
VIRTUAL_COUNT = 512
BLOCK = 128


def symmetric_matrix(key, order):
    raw = jax.random.normal(jax.random.fold_in(key, 11), (order, order), jnp.float32)
    matrix = (raw + raw.T) * 0.7071
    return (matrix * order ** (-0.5)).astype(jnp.bfloat16)


def block_mask(key, count):
    levels = jax.random.randint(jax.random.fold_in(key, 21), (count,), 30, 101)
    raw = jax.random.randint(jax.random.fold_in(key, 22), (count, count), 0, 100)
    places = jnp.arange(count)
    paired = jnp.where(places[:, None] <= places[None, :], raw, raw.T)
    limits = jnp.minimum(levels[:, None], levels[None, :])
    mask = (paired < limits).astype(jnp.int32)
    return jnp.maximum(mask, jnp.eye(count, dtype=jnp.int32))


def draw_ladder_operator(key, part):
    return symmetric_matrix(jax.random.fold_in(key, 1), VIRTUAL_SLAB * VIRTUAL_COUNT)


def draw_cycle_op(key, part):
    return symmetric_matrix(jax.random.fold_in(key, 2), OCCUPIED_SECOND * VIRTUAL_COUNT)


def draw_ladder_block_mask(key, part):
    return block_mask(jax.random.fold_in(key, 3), VIRTUAL_SLAB * VIRTUAL_COUNT // BLOCK)


def draw_cycle_mask(key, part):
    return block_mask(jax.random.fold_in(key, 4), OCCUPIED_SECOND * VIRTUAL_COUNT // BLOCK)


def block_scale(stream_key, shape, pieces, least, largest):
    loudness, own = 1.0, jax.random.fold_in(stream_key, 6)
    for position, blocks in pieces:
        heights = jnp.exp(jax.random.uniform(jax.random.fold_in(own, position), (blocks,), jnp.float32, least / len(pieces), largest / len(pieces)))
        loudness = loudness * jnp.repeat(heights, shape[position] // blocks).reshape([-1 if axis == position else 1 for axis in range(len(shape))])
    return loudness


def bell_draw(own_key, shape, scale, bound, cuts=(), kind=jnp.bfloat16):
    drawn = scale * jax.random.normal(own_key, shape, jnp.float32)
    if cuts:
        drawn = drawn * block_scale(own_key, shape, cuts, -0.22, 0.18)
    return jnp.clip(drawn, -bound, bound).astype(kind)


def setup_inputs(seed: int = 0) -> dict:
    keys = jax.random.split(jax.random.key(seed), 11)
    amps = bell_draw(keys[0], (OCCUPIED_FIRST, OCCUPIED_SECOND, VIRTUAL_SLAB, VIRTUAL_COUNT), 1.0, 6.0, ((1, 32), (2, 8)))
    driver = bell_draw(keys[1], (OCCUPIED_FIRST, OCCUPIED_SECOND, VIRTUAL_SLAB, VIRTUAL_COUNT), 1.0, 6.0, ((1, 8), (2, 32)))
    ladder_operator = draw_ladder_operator(jax.random.fold_in(keys[10], 71), 0)
    ladder_block_mask = draw_ladder_block_mask(jax.random.fold_in(keys[10], 71), 0)
    cycle_op = draw_cycle_op(jax.random.fold_in(keys[10], 71), 0)
    cycle_mask = draw_cycle_mask(jax.random.fold_in(keys[10], 71), 0)
    occ_i = jnp.clip(jax.random.uniform(keys[6], (OCCUPIED_FIRST,), jnp.float32, -2.0, -0.3), -2.0, -0.3)
    occ_j = jnp.clip(jax.random.uniform(keys[7], (OCCUPIED_SECOND,), jnp.float32, -2.0, -0.3), -2.0, -0.3)
    vir_a = jnp.clip(jax.random.uniform(keys[8], (VIRTUAL_SLAB,), jnp.float32, 0.2, 3.0), 0.2, 3.0)
    vir_b = jnp.clip(jax.random.uniform(keys[9], (VIRTUAL_COUNT,), jnp.float32, 0.2, 3.0), 0.2, 3.0)
    return dict(amps=amps, driver=driver, ladder_operator=ladder_operator, ladder_block_mask=ladder_block_mask, cycle_op=cycle_op, cycle_mask=cycle_mask, occ_i=occ_i, occ_j=occ_j, vir_a=vir_a, vir_b=vir_b)


def masked_operator(operator, mask):
    count = mask.shape[0]
    edge = operator.shape[0] // count
    shaped = operator.reshape(count, edge, count, edge)
    return (shaped * mask[:, None, :, None].astype(operator.dtype)).reshape(operator.shape)


def reference(amps, driver, ladder_operator, ladder_block_mask, cycle_op, cycle_mask, occ_i, occ_j, vir_a, vir_b):
    virtual_mask = masked_operator(ladder_operator, ladder_block_mask)
    wmask = masked_operator(cycle_op, cycle_mask)
    denom = (vir_a[None, None, :, None] + vir_b[None, None, None, :]
             - occ_i[:, None, None, None] - occ_j[None, :, None, None])

    def residual(doubles_amplitude):
        ladder_term = jnp.dot(doubles_amplitude.reshape(OCCUPIED_FIRST * OCCUPIED_SECOND, VIRTUAL_SLAB * VIRTUAL_COUNT), virtual_mask, preferred_element_type=jnp.float32)
        ladder_term = ladder_term.reshape(OCCUPIED_FIRST, OCCUPIED_SECOND, VIRTUAL_SLAB, VIRTUAL_COUNT)
        regrouped = jnp.transpose(doubles_amplitude, (0, 2, 1, 3)).reshape(OCCUPIED_FIRST * VIRTUAL_SLAB, OCCUPIED_SECOND * VIRTUAL_COUNT)
        cycle = jnp.dot(regrouped, wmask, preferred_element_type=jnp.float32)
        cycle = jnp.transpose(cycle.reshape(OCCUPIED_FIRST, VIRTUAL_SLAB, OCCUPIED_SECOND, VIRTUAL_COUNT), (0, 2, 1, 3))
        return ladder_term + cycle

    amp_one = (driver.astype(jnp.float32) + residual(amps)) / denom
    amp_rounded = amp_one.astype(jnp.bfloat16)
    amp_two = residual(amp_rounded) / denom
    return amp_one, amp_two
```

```python
import jax
import jax.numpy as jnp
from jax import lax
from jax.experimental import pallas as pl
from jax.experimental.pallas import tpu as pltpu
from jax.sharding import Mesh
from jax.sharding import PartitionSpec as P


AXES = ("sec", "rx", "core", "y", "zh")
WIDE = ("sec", "rx", "core")
COLS = ("y", "zh")
F32 = jnp.float32
BF16 = jnp.bfloat16
SHIFTS = (1, 3, 2)
FLIPS = (1, 2, 3)


def shifted(x, axis, step):
    n = lax.axis_size(axis)
    return lax.ppermute(x, axis, [(i, (i + step) % n) for i in range(n)])


def flipped(x, axis, mask):
    n = lax.axis_size(axis)
    return lax.ppermute(x, axis, [(i, i ^ mask) for i in range(n)])


def vmem(n):
    return [pl.BlockSpec(memory_space=pltpu.VMEM)] * n


def smem(n):
    return [pl.BlockSpec(memory_space=pltpu.SMEM)] * n


def sds(shape, dtype):
    return jax.ShapeDtypeStruct(shape, dtype)


def mask_tile(tile, mask):
    rows, cols = mask.shape
    edge_r = tile.shape[0] // rows
    edge_c = tile.shape[1] // cols

    def kernel(mask_ref, tile_ref, out_ref):
        for p in range(rows):
            for q in range(cols):
                at = (pl.ds(p * edge_r, edge_r), pl.ds(q * edge_c, edge_c))
                out_ref[at] = tile_ref[at] * mask_ref[p, q].astype(F32).astype(BF16)

    return pl.pallas_call(
        kernel,
        out_shape=sds(tile.shape, tile.dtype),
        in_specs=smem(1) + vmem(1),
        out_specs=vmem(1)[0],
        name="mask_tile",
    )(mask, tile)


def joined(parts):
    def kernel(*refs):
        out = refs[-1]
        for n, ref in enumerate(refs[:-1]):
            out[n] = ref[...]

    return pl.pallas_call(
        kernel,
        out_shape=sds((len(parts), *parts[0].shape), parts[0].dtype),
        in_specs=vmem(len(parts)),
        out_specs=vmem(1)[0],
        name="joined",
    )(*parts)


def dot(rows, tile, transposed):
    dims = (((1,), (1 if transposed else 0,)), ((), ()))
    return lax.dot_general(rows, tile, dims, preferred_element_type=F32)


def wide_product(place, parts, tile, transposed, wire):
    _, r_count, i_count, d_count = parts[0][0].shape
    flat = [ref for pair in parts for ref in pair]
    n_cols = tile.shape[0] if transposed else tile.shape[1]

    def kernel(place_ref, *refs):
        ins = refs[:8]
        tile_ref = refs[8]
        outs = refs[9:13]
        rows_ref = refs[13]
        z, x, core = place_ref[0], place_ref[1], place_ref[2]
        y, zh = place_ref[3], place_ref[4]
        for s in range(4):
            xs = (x + 4 - s) % 4
            for p in range(2):
                ref = ins[2 * s + p]
                cs = core ^ p
                for m in range(4):
                    zs = z ^ m
                    at = (((zs + 4 - y) % 4) * 2 + ((xs // 2) ^ zh)) * 4 + (xs % 2) * 2 + cs
                    for r in range(r_count):
                        rows_ref[r, at] = ref[m, r]
        acc = None
        for r in range(r_count):
            rows = rows_ref[r].reshape(32 * i_count, d_count)
            cut = pl.ds(r * d_count, d_count)
            part = dot(rows, tile_ref[:, cut] if transposed else tile_ref[cut, :], transposed)
            acc = part if acc is None else acc + part
        acc = acc.reshape(4, 2, 4, i_count, n_cols)
        for s in range(4):
            outs[s][...] = acc[s].astype(outs[s].dtype)

    shape = (2, 4, i_count, n_cols)
    return pl.pallas_call(
        kernel,
        out_shape=[sds(shape, F32 if s == 0 else wire) for s in range(4)],
        in_specs=smem(1) + vmem(9),
        out_specs=vmem(4),
        scratch_shapes=[pltpu.VMEM((r_count, 32, i_count, d_count), BF16)],
        name="wide_product",
    )(place, *flat, tile)


def cols_product(place, parts, tile, transposed, wire):
    r_count, i_count, d_count = parts[0][0].shape
    flat = [ref for pair in parts for ref in pair]
    tiles = (tile.shape[0] if transposed else tile.shape[1]) // d_count

    def kernel(place_ref, *refs):
        ins = refs[:8]
        tile_ref = refs[8]
        mine, other = refs[9:11]
        rows_ref = refs[11]
        z, x, core = place_ref[0], place_ref[1], place_ref[2]
        y, zh = place_ref[3], place_ref[4]
        for s in range(4):
            ys = (y + 4 - s) % 4
            for q in range(2):
                ref = ins[2 * s + q]
                for r in range(r_count):
                    xs = (zh ^ q) * 2 + r // 2
                    at = ((r % 2) ^ core) * 16 + ((xs + 4 - x) % 4) * 4 + (ys ^ z)
                    rows_ref[at] = ref[r]
        rows = rows_ref[...].reshape(32 * i_count, d_count)
        for n in range(tiles):
            cut = pl.ds(n * d_count, d_count)
            part = dot(rows, tile_ref[cut, :] if transposed else tile_ref[:, cut], transposed)
            part = part.reshape(2, 4, 4, i_count, d_count)
            mine[:, :, n] = part[0].astype(mine.dtype)
            other[:, :, n] = part[1].astype(other.dtype)

    shape = (4, 4, tiles, i_count, d_count)
    return pl.pallas_call(
        kernel,
        out_shape=[sds(shape, F32), sds(shape, wire)],
        in_specs=smem(1) + vmem(9),
        out_specs=vmem(2),
        scratch_shapes=[pltpu.VMEM((32, i_count, d_count), BF16)],
        name="cols_product",
    )(place, *flat, tile)


def summed(arrays, wire):
    count = arrays[0].shape[0]
    inside = arrays[0].shape[1:]

    def kernel(*refs):
        ins = refs[: len(arrays)]
        outs = refs[len(arrays) :]
        for n in range(count):
            total = ins[0][n].astype(F32)
            for ref in ins[1:]:
                total = total + ref[n].astype(F32)
            outs[n][...] = total.astype(outs[n].dtype)

    return pl.pallas_call(
        kernel,
        out_shape=[sds(inside, F32 if n == 0 else wire) for n in range(count)],
        in_specs=vmem(len(arrays)),
        out_specs=vmem(count),
        name="summed",
    )(*arrays)


def finished(arrays, denom, dtypes):
    def kernel(*refs):
        ins = refs[: len(arrays)]
        denom_ref = refs[len(arrays)]
        outs = refs[len(arrays) + 1 :]
        total = ins[0][...].astype(F32)
        for ref in ins[1:]:
            total = total + ref[...].astype(F32)
        total = total / denom_ref[...]
        for out in outs:
            out[...] = total.astype(out.dtype)

    return pl.pallas_call(
        kernel,
        out_shape=[sds(denom.shape, dtype) for dtype in dtypes],
        in_specs=vmem(len(arrays) + 1),
        out_specs=vmem(len(dtypes)),
        name="finished",
    )(*arrays, denom)


def wide_gather(piece):
    parts = joined([piece] + [flipped(piece, "sec", m) for m in FLIPS])
    here = {0: parts}
    for s in SHIFTS:
        here[s] = shifted(parts, "rx", s)
    return [(here[s], flipped(here[s], "core", 1)) for s in range(4)]


def cols_gather(piece):
    pair = (piece, flipped(piece, "zh", 1))
    here = {0: pair}
    for s in SHIFTS:
        here[s] = tuple(shifted(one, "y", s) for one in pair)
    return [here[s] for s in range(4)]


def cols_sum(outs, wire):
    arrays = [outs[0]] + [shifted(outs[s], "y", s) for s in SHIFTS]
    mine, other = summed(arrays, wire)
    return [mine, flipped(other, "zh", 1)]


def wide_sum(mine, other, wire):
    parts = summed([mine, flipped(other, "core", 1)], wire)
    arrays = [parts[0]] + [shifted(parts[s], "rx", s) for s in SHIFTS]
    parts = summed(arrays, wire)
    return [parts[0]] + [flipped(parts[m], "sec", m) for m in FLIPS]


def sweep(piece, place, wide_tile, cols_tile, transposed, wire):
    wide_parts = wide_gather(piece)
    cols_parts = cols_gather(piece)
    mine, other = cols_product(place, cols_parts, cols_tile, transposed, wire)
    outs = wide_product(place, wide_parts, wide_tile, transposed, wire)
    return cols_sum(outs, wire) + wide_sum(mine, other, wire)


def body(
    amps,
    driver,
    ladder_operator,
    ladder_block_mask,
    cycle_op,
    cycle_mask,
    occ_i,
    occ_j,
    vir_a,
    vir_b,
):
    place = jnp.stack([lax.axis_index(name) for name in AXES]).astype(jnp.int32)
    wide_index = lax.axis_index(WIDE)
    cols_index = lax.axis_index(COLS)
    per_cols = amps.shape[2]
    ladder_tile = mask_tile(ladder_operator, ladder_block_mask)
    cycle_tile = mask_tile(cycle_op, cycle_mask)

    def denominator(occ_part, vir_part):
        return vir_part + vir_b[None, None, :] - occ_i[None, :, None] - occ_part

    occ_cols = lax.dynamic_slice_in_dim(occ_j, cols_index * per_cols, per_cols)[:, None, None]
    vir_cols = lax.dynamic_slice_in_dim(vir_a, cols_index * per_cols, per_cols)[:, None, None]
    occ_wide = lax.dynamic_slice_in_dim(occ_j, wide_index, 1)[:, None, None]
    vir_wide = lax.dynamic_slice_in_dim(vir_a, wide_index, 1)[:, None, None]
    denom_one = denominator(occ_cols, vir_wide)
    denom_two = denominator(occ_wide, vir_cols)

    piece = jnp.transpose(amps[:, 0], (1, 0, 2))
    base = jnp.transpose(driver[:, :, 0], (1, 0, 2))
    arrays = sweep(piece, place, ladder_tile, cycle_tile, False, F32)
    amp_one, amp_rounded = finished([base] + arrays, denom_one, (F32, BF16))
    arrays = sweep(amp_rounded, place, cycle_tile, ladder_tile, True, BF16)
    (amp_two,) = finished(arrays, denom_two, (F32,))
    return (
        jnp.transpose(amp_one, (1, 0, 2))[:, :, None],
        jnp.transpose(amp_two, (1, 0, 2))[:, None],
    )


def solution(mesh):
    split = Mesh(mesh.devices.reshape(4, 4, 2, 4, 2), AXES)
    return jax.shard_map(
        body,
        mesh=split,
        in_specs=(
            P(None, WIDE, COLS, None),
            P(None, COLS, WIDE, None),
            P(COLS, WIDE),
            P(COLS, WIDE),
            P(WIDE, COLS),
            P(WIDE, COLS),
            P(),
            P(),
            P(),
            P(),
        ),
        out_specs=(P(None, COLS, WIDE, None), P(None, WIDE, COLS, None)),
        check_vma=False,
    )
```

```python
import jax
import jax.numpy as jnp
from jax import lax
from jax.experimental import pallas as pl
from jax.experimental.pallas import tpu as pltpu
from jax.sharding import Mesh
from jax.sharding import PartitionSpec as P


AXES = ("sec", "rx", "core", "y", "zh")
WIDE = ("sec", "rx", "core")
COLS = ("y", "zh")
F32 = jnp.float32
BF16 = jnp.bfloat16
SHIFTS = (1, 3, 2)
FLIPS = (1, 2, 3)


def shifted(x, axis, step):
    n = lax.axis_size(axis)
    return lax.ppermute(x, axis, [(i, (i + step) % n) for i in range(n)])


def flipped(x, axis, mask):
    n = lax.axis_size(axis)
    return lax.ppermute(x, axis, [(i, i ^ mask) for i in range(n)])


def swapped(x, axes):
    n = 2 ** len(axes)
    return lax.ppermute(x, axes, [(i, n - 1 - i) for i in range(n)])


def vmem(n):
    return [pl.BlockSpec(memory_space=pltpu.VMEM)] * n


def smem(n):
    return [pl.BlockSpec(memory_space=pltpu.SMEM)] * n


LIMIT = pltpu.CompilerParams(vmem_limit_bytes=16 * 2**20)


def on_chip(*arrays):
    return [pltpu.with_memory_space_constraint(x, pltpu.VMEM) for x in arrays]


def sds(shape, dtype):
    return pltpu.VMEM(shape, dtype)


def mask_tile(tile, mask):
    rows, cols = mask.shape
    edge_r = tile.shape[0] // rows
    edge_c = tile.shape[1] // cols

    def kernel(mask_ref, tile_ref, out_ref):
        for p in range(rows):
            for q in range(cols):
                at = (pl.ds(p * edge_r, edge_r), pl.ds(q * edge_c, edge_c))
                out_ref[at] = tile_ref[at] * mask_ref[p, q].astype(F32).astype(BF16)

    return pl.pallas_call(
        kernel,
        out_shape=sds(tile.shape, tile.dtype),
        in_specs=smem(1) + vmem(1),
        out_specs=vmem(1)[0],
        compiler_params=LIMIT,
        name="mask_tile",
    )(mask, *on_chip(tile))


def joined(parts):
    def kernel(*refs):
        out = refs[-1]
        for n, ref in enumerate(refs[:-1]):
            out[n] = ref[...]

    return pl.pallas_call(
        kernel,
        out_shape=sds((len(parts), *parts[0].shape), parts[0].dtype),
        in_specs=vmem(len(parts)),
        out_specs=vmem(1)[0],
        compiler_params=LIMIT,
        name="joined",
    )(*on_chip(*parts))


def dot(rows, tile, transposed):
    dims = (((1,), (1 if transposed else 0,)), ((), ()))
    return lax.dot_general(rows, tile, dims, preferred_element_type=F32)


def wide_product(place, parts, tiles, transposed, wire):
    _, r_count, i_count, d_count = parts[0].shape
    n_cols = tiles[0].shape[0] if transposed else tiles[0].shape[1]

    def kernel(place_ref, *refs):
        ins = refs[:4]
        tile_refs = refs[4:6]
        outs = refs[6:10]
        rows_ref = refs[10]
        z, x = place_ref[0], place_ref[1]
        y, zh = place_ref[3], place_ref[4]
        for s in range(4):
            xs = (x + 4 - s) % 4
            for m in range(4):
                zs = z ^ m
                at = (((zs + 4 - y) % 4) * 2 + ((xs // 2) ^ zh)) * 2 + xs % 2
                for r in range(r_count):
                    rows_ref[r, at] = ins[s][m, r]
        for q in range(2):
            acc = None
            for r in range(r_count):
                rows = rows_ref[r].reshape(16 * i_count, d_count)
                cut = pl.ds(r * d_count, d_count)
                part = dot(rows, tile_refs[q][:, cut] if transposed else tile_refs[q][cut, :], transposed)
                acc = part if acc is None else acc + part
            acc = acc.reshape(4, 2, 2, i_count, n_cols)
            for s in range(4):
                outs[s][:, q] = acc[s].astype(outs[s].dtype)

    shape = (2, 2, 2, i_count, n_cols)
    return pl.pallas_call(
        kernel,
        out_shape=[sds(shape, F32 if s == 0 else wire) for s in range(4)],
        in_specs=smem(1) + vmem(6),
        out_specs=vmem(4),
        scratch_shapes=[pltpu.VMEM((r_count, 16, i_count, d_count), BF16)],
        compiler_params=LIMIT,
        name="wide_product",
    )(place, *on_chip(*parts, *tiles))


def cols_product(place, parts, tiles, transposed, wire):
    i_count, d_count = parts[0].shape[-2:]
    cuts = (tiles[0].shape[0] if transposed else tiles[0].shape[1]) // d_count

    def kernel(place_ref, *refs):
        ins = refs[:4]
        tile_refs = refs[4:6]
        outs = refs[6:10]
        rows_ref = refs[10]
        z, x = place_ref[0], place_ref[1]
        y, zh = place_ref[3], place_ref[4]
        for s in range(4):
            ys = (y + 4 - s) % 4
            for q in range(2):
                for half in range(2):
                    xs = (zh ^ q) * 2 + half
                    at = ((xs + 4 - x) % 4) * 4 + (ys ^ z)
                    for k in range(2):
                        rows_ref[k, at] = ins[s][q, k, half]
        for n in range(cuts):
            cut = pl.ds(n * d_count, d_count)
            acc = None
            for k in range(2):
                rows = rows_ref[k].reshape(16 * i_count, d_count)
                part = dot(rows, tile_refs[k][cut, :] if transposed else tile_refs[k][:, cut], transposed)
                acc = part if acc is None else acc + part
            acc = acc.reshape(4, 4, i_count, d_count)
            for s in range(4):
                outs[s][:, n] = acc[s].astype(outs[s].dtype)

    shape = (4, cuts, i_count, d_count)
    return pl.pallas_call(
        kernel,
        out_shape=[sds(shape, F32 if s == 0 else wire) for s in range(4)],
        in_specs=smem(1) + vmem(6),
        out_specs=vmem(4),
        scratch_shapes=[pltpu.VMEM((2, 16, i_count, d_count), BF16)],
        compiler_params=LIMIT,
        name="cols_product",
    )(place, *on_chip(*parts, *tiles))


def summed(arrays, wire, depth):
    lead = arrays[0].shape[:depth]
    inside = arrays[0].shape[depth:]
    places = [()]
    for size in lead:
        places = [at + (n,) for at in places for n in range(size)]

    def kernel(*refs):
        ins = refs[: len(arrays)]
        outs = refs[len(arrays) :]
        for out, at in zip(outs, places):
            total = ins[0][at].astype(F32)
            for ref in ins[1:]:
                total = total + ref[at].astype(F32)
            out[...] = total.astype(out.dtype)

    return pl.pallas_call(
        kernel,
        out_shape=[sds(inside, F32 if n == 0 else wire) for n in range(len(places))],
        in_specs=vmem(len(arrays)),
        out_specs=vmem(len(places)),
        compiler_params=LIMIT,
        name="summed",
    )(*on_chip(*arrays))


def finished(place, whole, near, far, denom, onward):
    n_whole, n_near = len(whole), len(near)

    def kernel(place_ref, *refs):
        wholes = refs[:n_whole]
        halves = (refs[n_whole : n_whole + n_near], refs[n_whole + n_near : n_whole + 2 * n_near])
        denom_ref = refs[n_whole + 2 * n_near]
        outs = refs[n_whole + 2 * n_near + 1 :]
        core = place_ref[2]
        for k in range(2):
            for half in range(2):
                r = half * 2 + (core ^ k)
                total = wholes[0][r].astype(F32)
                for ref in wholes[1:]:
                    total = total + ref[r].astype(F32)
                for ref in halves[k]:
                    total = total + ref[half].astype(F32)
                total = total / denom_ref[r]
                outs[0][r] = total
                if onward:
                    rounded = total.astype(BF16)
                    outs[1][r] = rounded
                    outs[2 + k][half] = rounded

    shapes = [sds(denom.shape, F32)]
    if onward:
        shapes += [sds(denom.shape, BF16)] + [sds((denom.shape[0] // 2, *denom.shape[1:]), BF16)] * 2
    return pl.pallas_call(
        kernel,
        out_shape=shapes,
        in_specs=smem(1) + vmem(n_whole + 2 * n_near + 1),
        out_specs=vmem(len(shapes)),
        compiler_params=LIMIT,
        name="finished",
    )(place, *on_chip(*whole, *near, *far, denom))


def prepared(place, amps):
    i_count, r_count, d_count = amps.shape

    def kernel(place_ref, in_ref, all_ref, near_ref, far_ref):
        core = place_ref[2]
        for r in range(r_count):
            all_ref[r] = in_ref[:, r, :]
        for half in range(r_count // 2):
            near_ref[half] = all_ref[half * 2 + core]
            far_ref[half] = all_ref[half * 2 + (core ^ 1)]

    return pl.pallas_call(
        kernel,
        out_shape=[sds((r_count, i_count, d_count), BF16)] + [sds((r_count // 2, i_count, d_count), BF16)] * 2,
        in_specs=smem(1) + vmem(1),
        out_specs=vmem(3),
        compiler_params=LIMIT,
        name="prepared",
    )(place, *on_chip(amps))


def wide_gather(piece):
    parts = joined([piece] + [flipped(piece, "sec", m) for m in FLIPS])
    here = {0: parts}
    for s in SHIFTS:
        here[s] = shifted(parts, "rx", s)
    return [here[s] for s in range(4)]


def cols_gather(near, far):
    zh = swapped(near, ("zh",))
    both = swapped(far, ("core", "zh"))
    core = swapped(far, ("core",))
    parts = joined([near, core, zh, both])
    parts = parts.reshape(2, 2, *parts.shape[1:])
    here = {0: parts}
    for s in SHIFTS:
        here[s] = shifted(parts, "y", s)
    return [here[s] for s in range(4)]


def cols_sum(outs, wire):
    arrays = [outs[0]] + [shifted(outs[s], "y", s) for s in SHIFTS]
    own, core, zh, both = summed(arrays, wire, 2)
    near = [own, swapped(zh, ("zh",))]
    far = [swapped(core, ("core",)), swapped(both, ("core", "zh"))]
    return near, far


def wide_sum(outs, wire):
    arrays = [outs[0]] + [shifted(outs[s], "rx", s) for s in SHIFTS]
    parts = summed(arrays, wire, 1)
    return [parts[0]] + [flipped(parts[m], "sec", m) for m in FLIPS]


def sweep(piece, near, far, place, wide_tiles, cols_tiles, transposed, wire):
    wide_parts = wide_gather(piece)
    cols_parts = cols_gather(near, far)
    outs = cols_product(place, cols_parts, cols_tiles, transposed, wire)
    whole = wide_sum(outs, wire)
    outs = wide_product(place, wide_parts, wide_tiles, transposed, wire)
    near, far = cols_sum(outs, wire)
    return whole, near, far


def body(
    amps,
    driver,
    ladder_operator,
    ladder_block_mask,
    cycle_op,
    cycle_mask,
    occ_i,
    occ_j,
    vir_a,
    vir_b,
):
    place = jnp.stack([lax.axis_index(name) for name in AXES]).astype(jnp.int32)
    wide_index = lax.axis_index(WIDE)
    cols_index = lax.axis_index(COLS)
    per_cols = amps.shape[2]

    def denominator(occ_part, vir_part):
        return vir_part + vir_b[None, None, :] - occ_i[None, :, None] - occ_part

    occ_cols = lax.dynamic_slice_in_dim(occ_j, cols_index * per_cols, per_cols)[:, None, None]
    vir_cols = lax.dynamic_slice_in_dim(vir_a, cols_index * per_cols, per_cols)[:, None, None]
    occ_wide = lax.dynamic_slice_in_dim(occ_j, wide_index, 1)[:, None, None]
    vir_wide = lax.dynamic_slice_in_dim(vir_a, wide_index, 1)[:, None, None]
    denom_one = denominator(occ_cols, vir_wide)
    denom_two = denominator(occ_wide, vir_cols)

    base = jnp.transpose(driver[:, :, 0], (1, 0, 2))
    start = prepared(place, amps[:, 0])
    cycle_tile = mask_tile(cycle_op, cycle_mask)
    ladder_tile = mask_tile(ladder_operator, ladder_block_mask)
    cycle_tiles = (cycle_tile, swapped(cycle_tile, ("core",)))
    ladder_tiles = (ladder_tile, swapped(ladder_tile, ("core",)))
    whole, near, far = sweep(*start, place, ladder_tiles, cycle_tiles, False, F32)
    amp_one, *start = finished(place, [base] + whole, near, far, denom_one, True)
    whole, near, far = sweep(*start, place, cycle_tiles, ladder_tiles, True, BF16)
    (amp_two,) = finished(place, whole, near, far, denom_two, False)
    return (
        jnp.transpose(amp_one, (1, 0, 2))[:, :, None],
        jnp.transpose(amp_two, (1, 0, 2))[:, None],
    )


def solution(mesh):
    split = Mesh(mesh.devices.reshape(4, 4, 2, 4, 2), AXES)
    return jax.shard_map(
        body,
        mesh=split,
        in_specs=(
            P(None, WIDE, COLS, None),
            P(None, COLS, WIDE, None),
            P(COLS, WIDE),
            P(COLS, WIDE),
            P(WIDE, COLS),
            P(WIDE, COLS),
            P(),
            P(),
            P(),
            P(),
        ),
        out_specs=(P(None, COLS, WIDE, None), P(None, WIDE, COLS, None)),
        check_vma=False,
    )
```

```python
import jax
import jax.numpy as jnp
from jax import lax
from jax.experimental import pallas as pl
from jax.experimental.pallas import tpu as pltpu
from jax.sharding import Mesh
from jax.sharding import PartitionSpec as P


AXES = ("sec", "rx", "core", "y", "zh")
WIDE = ("sec", "rx", "core")
COLS = ("y", "zh")
F32 = jnp.float32
BF16 = jnp.bfloat16
SHIFTS = (1, 3, 2)
FLIPS = (1, 2, 3)


def shifted(x, axis, step):
    n = lax.axis_size(axis)
    return lax.ppermute(x, axis, [(i, (i + step) % n) for i in range(n)])


def flipped(x, axis, mask):
    n = lax.axis_size(axis)
    return lax.ppermute(x, axis, [(i, i ^ mask) for i in range(n)])


def swapped(x, axes):
    n = 2 ** len(axes)
    return lax.ppermute(x, axes, [(i, n - 1 - i) for i in range(n)])


def vmem(n):
    return [pl.BlockSpec(memory_space=pltpu.VMEM)] * n


def smem(n):
    return [pl.BlockSpec(memory_space=pltpu.SMEM)] * n


LIMIT = pltpu.CompilerParams(vmem_limit_bytes=16 * 2**20)


def on_chip(*arrays):
    return [pltpu.with_memory_space_constraint(x, pltpu.VMEM) for x in arrays]


def sds(shape, dtype):
    return pltpu.VMEM(shape, dtype)


def mask_tile(tile, mask, turned):
    rows, cols = mask.shape
    edge_r = tile.shape[0] // rows
    edge_c = tile.shape[1] // cols

    def kernel(mask_ref, tile_ref, out_ref):
        p = pl.program_id(0)
        start = pl.multiple_of(p * edge_r, edge_r)
        for q in range(cols):
            cut = pl.ds(q * edge_c, edge_c)
            value = mask_ref[q, p] if turned else mask_ref[p, q]
            out_ref[pl.ds(start, edge_r), cut] = tile_ref[:, cut] * value.astype(F32).astype(BF16)

    return pl.pallas_call(
        kernel,
        grid=(rows,),
        out_shape=sds(tile.shape, tile.dtype),
        in_specs=smem(1) + [pl.BlockSpec((edge_r, tile.shape[1]), lambda p: (p, 0))],
        out_specs=vmem(1)[0],
        compiler_params=LIMIT,
        name="mask_tile",
    )(mask.T if turned else mask, tile)


def joined(parts):
    def kernel(*refs):
        out = refs[-1]
        for n, ref in enumerate(refs[:-1]):
            out[n] = ref[...]

    return pl.pallas_call(
        kernel,
        out_shape=sds((len(parts), *parts[0].shape), parts[0].dtype),
        in_specs=vmem(len(parts)),
        out_specs=vmem(1)[0],
        compiler_params=LIMIT,
        name="joined",
    )(*on_chip(*parts))


def dot(rows, tile, transposed):
    dims = (((1,), (1 if transposed else 0,)), ((), ()))
    return lax.dot_general(rows, tile, dims, preferred_element_type=F32)


def place():
    return [lax.axis_index(name) for name in AXES]


def wide_product(parts, tiles, transposed, wire):
    _, r_count, i_count, d_count = parts[0].shape
    n_cols = tiles[0].shape[0] if transposed else tiles[0].shape[1]

    def kernel(*refs):
        ins = refs[:4]
        tile_refs = refs[4:6]
        outs = refs[6:10]
        rows_ref = refs[10]
        z, x, _, y, zh = place()
        for s in range(4):
            xs = (x + 4 - s) % 4
            for m in range(4):
                zs = z ^ m
                at = (((zs + 4 - y) % 4) * 2 + ((xs // 2) ^ zh)) * 2 + xs % 2
                for r in range(r_count):
                    rows_ref[r, at] = ins[s][m, r]
        for q in range(2):
            acc = None
            for r in range(r_count):
                rows = rows_ref[r].reshape(16 * i_count, d_count)
                cut = pl.ds(r * d_count, d_count)
                part = dot(rows, tile_refs[q][:, cut] if transposed else tile_refs[q][cut, :], transposed)
                acc = part if acc is None else acc + part
            acc = acc.reshape(4, 2, 2, i_count, n_cols)
            for s in range(4):
                outs[s][:, q] = acc[s].astype(outs[s].dtype)

    shape = (2, 2, 2, i_count, n_cols)
    return pl.pallas_call(
        kernel,
        out_shape=[sds(shape, F32 if s == 0 else wire) for s in range(4)],
        in_specs=vmem(6),
        out_specs=vmem(4),
        scratch_shapes=[pltpu.VMEM((r_count, 16, i_count, d_count), BF16)],
        compiler_params=LIMIT,
        name="wide_product",
    )(*on_chip(*parts, *tiles))


def cols_product(parts, tiles, transposed, wire):
    i_count, d_count = parts[0].shape[-2:]
    cuts = (tiles[0].shape[0] if transposed else tiles[0].shape[1]) // d_count

    def kernel(*refs):
        ins = refs[:4]
        tile_refs = refs[4:6]
        outs = refs[6:10]
        rows_ref = refs[10]
        z, x, _, y, zh = place()
        for s in range(4):
            ys = (y + 4 - s) % 4
            for q in range(2):
                for half in range(2):
                    xs = (zh ^ q) * 2 + half
                    at = ((xs + 4 - x) % 4) * 4 + (ys ^ z)
                    for k in range(2):
                        rows_ref[k, at] = ins[s][q, k, half]

        @pl.loop(0, cuts)
        def _(n):
            cut = pl.ds(pl.multiple_of(n * d_count, d_count), d_count)
            acc = None
            for k in range(2):
                rows = rows_ref[k].reshape(16 * i_count, d_count)
                part = dot(rows, tile_refs[k][cut, :] if transposed else tile_refs[k][:, cut], transposed)
                acc = part if acc is None else acc + part
            acc = acc.reshape(4, 4, i_count, d_count)
            for s in range(4):
                outs[s][:, n] = acc[s].astype(outs[s].dtype)

    shape = (4, cuts, i_count, d_count)
    return pl.pallas_call(
        kernel,
        out_shape=[sds(shape, F32 if s == 0 else wire) for s in range(4)],
        in_specs=vmem(6),
        out_specs=vmem(4),
        scratch_shapes=[pltpu.VMEM((2, 16, i_count, d_count), BF16)],
        compiler_params=LIMIT,
        name="cols_product",
    )(*on_chip(*parts, *tiles))


def summed(arrays, wire, depth):
    lead = arrays[0].shape[:depth]
    inside = arrays[0].shape[depth:]
    places = [()]
    for size in lead:
        places = [at + (n,) for at in places for n in range(size)]

    def kernel(*refs):
        ins = refs[: len(arrays)]
        outs = refs[len(arrays) :]
        for out, at in zip(outs, places):
            total = ins[0][at].astype(F32)
            for ref in ins[1:]:
                total = total + ref[at].astype(F32)
            out[...] = total.astype(out.dtype)

    return pl.pallas_call(
        kernel,
        out_shape=[sds(inside, F32 if n == 0 else wire) for n in range(len(places))],
        in_specs=vmem(len(arrays)),
        out_specs=vmem(len(places)),
        compiler_params=LIMIT,
        name="summed",
    )(*on_chip(*arrays))


def finished(base, whole, near, far, energies, swap, onward):
    n_base, n_whole, n_near = len(base), len(whole), len(near)
    r_count, i_count, d_count = whole[0].shape

    def kernel(*refs):
        refs = list(refs)

        def take(n):
            taken = refs[:n]
            del refs[:n]
            return taken

        occ_i, occ_j, vir_a, vir_b = take(4)
        bases, wholes, halves = take(n_base), take(n_whole), (take(n_near), take(n_near))
        outs, (stage,) = take(len(shapes)), take(1)
        z, x, core, y, zh = place()
        wide, cols = (z * 4 + x) * 2 + core, y * 2 + zh
        row = lax.broadcasted_iota(jnp.int32, (i_count, d_count), 0)
        occ = jnp.zeros((i_count, d_count), F32)
        for i in range(i_count):
            occ = jnp.where(row == i, occ_i[i], occ)
        for ref in bases:
            for r in range(r_count):
                stage[r] = ref[:, r, :].astype(F32)
        for k in range(2):
            for half in range(2):
                r = half * 2 + (core ^ k)
                total = wholes[0][r].astype(F32)
                for ref in wholes[1:]:
                    total = total + ref[r].astype(F32)
                for ref in halves[k]:
                    total = total + ref[half].astype(F32)
                if n_base:
                    total = total + stage[r]
                place_j, place_a = (cols * r_count + r, wide) if swap else (wide, cols * r_count + r)
                total = total / (vir_a[place_a] + vir_b[...] - occ - occ_j[place_j])
                stage[r] = total
                if onward:
                    rounded = total.astype(BF16)
                    outs[1][r] = rounded
                    outs[2 + k][half] = rounded
        for r in range(r_count):
            outs[0][:, r, :] = stage[r]

    shapes = [jax.ShapeDtypeStruct((i_count, r_count, d_count), F32)]
    if onward:
        shapes += [sds((r_count, i_count, d_count), BF16)] + [sds((r_count // 2, i_count, d_count), BF16)] * 2
    return pl.pallas_call(
        kernel,
        out_shape=shapes,
        in_specs=smem(3) + vmem(n_base + n_whole + 2 * n_near + 1),
        out_specs=vmem(len(shapes)),
        scratch_shapes=[pltpu.VMEM((r_count, i_count, d_count), F32)],
        compiler_params=LIMIT,
        name="finished",
    )(*energies[:3], *on_chip(energies[3][None], *base, *whole, *near, *far))


def prepared(amps):
    i_count, r_count, d_count = amps.shape

    def kernel(in_ref, all_ref, near_ref, far_ref):
        core = lax.axis_index("core")
        for r in range(r_count):
            all_ref[r] = in_ref[:, r, :]
        for half in range(r_count // 2):
            near_ref[half] = all_ref[half * 2 + core]
            far_ref[half] = all_ref[half * 2 + (core ^ 1)]

    return pl.pallas_call(
        kernel,
        out_shape=[sds((r_count, i_count, d_count), BF16)] + [sds((r_count // 2, i_count, d_count), BF16)] * 2,
        in_specs=vmem(1),
        out_specs=vmem(3),
        compiler_params=LIMIT,
        name="prepared",
    )(*on_chip(amps))


def wide_gather(piece):
    parts = joined([piece] + [flipped(piece, "sec", m) for m in FLIPS])
    here = {0: parts}
    for s in SHIFTS:
        here[s] = shifted(parts, "rx", s)
    return [here[s] for s in range(4)]


def cols_gather(near, far):
    zh = swapped(near, ("zh",))
    both = swapped(far, ("core", "zh"))
    core = swapped(far, ("core",))
    parts = joined([near, core, zh, both])
    parts = parts.reshape(2, 2, *parts.shape[1:])
    here = {0: parts}
    for s in SHIFTS:
        here[s] = shifted(parts, "y", s)
    return [here[s] for s in range(4)]


def cols_sum(outs, wire):
    arrays = [outs[0]] + [shifted(outs[s], "y", s) for s in SHIFTS]
    own, core, zh, both = summed(arrays, wire, 2)
    near = [own, swapped(zh, ("zh",))]
    far = [swapped(core, ("core",)), swapped(both, ("core", "zh"))]
    return near, far


def wide_sum(outs, wire):
    arrays = [outs[0]] + [shifted(outs[s], "rx", s) for s in SHIFTS]
    parts = summed(arrays, wire, 1)
    return [parts[0]] + [flipped(parts[m], "sec", m) for m in FLIPS]


def sweep(piece, near, far, wide_tiles, cols_tiles, transposed, wire):
    wide_parts = wide_gather(piece)
    cols_parts = cols_gather(near, far)
    outs = cols_product(cols_parts, cols_tiles, transposed, wire)
    whole = wide_sum(outs, wire)
    outs = wide_product(wide_parts, wide_tiles, transposed, wire)
    near, far = cols_sum(outs, wire)
    return whole, near, far


def body(
    amps,
    driver,
    ladder_operator,
    ladder_block_mask,
    cycle_op,
    cycle_mask,
    occ_i,
    occ_j,
    vir_a,
    vir_b,
):
    energies = (occ_i, occ_j, vir_a, vir_b)
    start = prepared(amps[:, 0])
    cycle_tile = mask_tile(cycle_op, cycle_mask, False)
    ladder_tile = mask_tile(ladder_operator, ladder_block_mask, True)
    cycle_tiles = (cycle_tile, swapped(cycle_tile, ("core",)))
    ladder_tiles = (ladder_tile, swapped(ladder_tile, ("core",)))
    sums = sweep(*start, ladder_tiles, cycle_tiles, False, F32)
    amp_one, *start = finished([driver[:, :, 0]], *sums, energies, True, True)
    sums = sweep(*start, cycle_tiles, ladder_tiles, True, BF16)
    (amp_two,) = finished([], *sums, energies, False, False)
    return amp_one[:, :, None], amp_two[:, None]


def solution(mesh):
    split = Mesh(mesh.devices.reshape(4, 4, 2, 4, 2), AXES)
    return jax.shard_map(
        body,
        mesh=split,
        in_specs=(
            P(None, WIDE, COLS, None),
            P(None, COLS, WIDE, None),
            P(COLS, WIDE),
            P(COLS, WIDE),
            P(WIDE, COLS),
            P(WIDE, COLS),
            P(),
            P(),
            P(),
            P(),
        ),
        out_specs=(P(None, COLS, WIDE, None), P(None, WIDE, COLS, None)),
        check_vma=False,
    )
```

```python
import jax
import jax.numpy as jnp
from jax import lax
from jax.experimental import pallas as pl
from jax.experimental.pallas import tpu as pltpu
from jax.sharding import Mesh
from jax.sharding import PartitionSpec as P


AXES = ("sec", "rx", "core", "y", "zh")
WIDE = ("sec", "rx", "core")
COLS = ("y", "zh")
F32 = jnp.float32
BF16 = jnp.bfloat16
SHIFTS = (1, 3, 2)
FLIPS = (1, 2, 3)


def shifted(x, axis, step):
    n = lax.axis_size(axis)
    return lax.ppermute(x, axis, [(i, (i + step) % n) for i in range(n)])


def flipped(x, axis, mask):
    n = lax.axis_size(axis)
    return lax.ppermute(x, axis, [(i, i ^ mask) for i in range(n)])


def swapped(x, axes):
    n = 2 ** len(axes)
    return lax.ppermute(x, axes, [(i, n - 1 - i) for i in range(n)])


def vmem(n):
    return [pl.BlockSpec(memory_space=pltpu.VMEM)] * n


def smem(n):
    return [pl.BlockSpec(memory_space=pltpu.SMEM)] * n


LIMIT = pltpu.CompilerParams(vmem_limit_bytes=16 * 2**20)


def on_chip(*arrays):
    return [pltpu.with_memory_space_constraint(x, pltpu.VMEM) for x in arrays]


def sds(shape, dtype):
    return pltpu.VMEM(shape, dtype)


def mask_tile(tile, mask, turned):
    rows, cols = mask.shape
    edge_r = tile.shape[0] // rows
    edge_c = tile.shape[1] // cols

    def kernel(mask_ref, tile_ref, out_ref):
        @pl.loop(0, rows)
        def _(p):
            down = pl.ds(pl.multiple_of(p * edge_r, edge_r), edge_r)
            for q in range(cols):
                cut = pl.ds(q * edge_c, edge_c)
                value = mask_ref[q, p] if turned else mask_ref[p, q]
                out_ref[down, cut] = tile_ref[down, cut] * value.astype(F32).astype(BF16)

    return pl.pallas_call(
        kernel,
        out_shape=sds(tile.shape, tile.dtype),
        in_specs=smem(1) + vmem(1),
        out_specs=vmem(1)[0],
        compiler_params=LIMIT,
        name="mask_tile",
    )(mask.T if turned else mask, tile)


def joined(parts):
    def kernel(*refs):
        out = refs[-1]
        for n, ref in enumerate(refs[:-1]):
            out[n] = ref[...]

    return pl.pallas_call(
        kernel,
        out_shape=sds((len(parts), *parts[0].shape), parts[0].dtype),
        in_specs=vmem(len(parts)),
        out_specs=vmem(1)[0],
        compiler_params=LIMIT,
        name="joined",
    )(*on_chip(*parts))


def dot(rows, tile, transposed):
    dims = (((1,), (1 if transposed else 0,)), ((), ()))
    return lax.dot_general(rows, tile, dims, preferred_element_type=F32)


def place():
    return [lax.axis_index(name) for name in AXES]


def wide_product(parts, tiles, transposed, wire):
    _, r_count, i_count, d_count = parts[0].shape
    n_cols = tiles[0].shape[0] if transposed else tiles[0].shape[1]

    def kernel(*refs):
        ins = refs[:4]
        tile_refs = refs[4:6]
        outs = refs[6:10]
        rows_ref = refs[10]
        z, x, _, y, zh = place()
        for s in range(4):
            xs = (x + 4 - s) % 4
            for m in range(4):
                zs = z ^ m
                at = (((zs + 4 - y) % 4) * 2 + ((xs // 2) ^ zh)) * 2 + xs % 2
                for r in range(r_count):
                    rows_ref[r, at] = ins[s][m, r]
        for q in range(2):
            acc = None
            for r in range(r_count):
                rows = rows_ref[r].reshape(16 * i_count, d_count)
                cut = pl.ds(r * d_count, d_count)
                part = dot(rows, tile_refs[q][:, cut] if transposed else tile_refs[q][cut, :], transposed)
                acc = part if acc is None else acc + part
            acc = acc.reshape(4, 2, 2, i_count, n_cols)
            for s in range(4):
                outs[s][:, q] = acc[s].astype(outs[s].dtype)

    shape = (2, 2, 2, i_count, n_cols)
    return pl.pallas_call(
        kernel,
        out_shape=[sds(shape, F32 if s == 0 else wire) for s in range(4)],
        in_specs=vmem(6),
        out_specs=vmem(4),
        scratch_shapes=[pltpu.VMEM((r_count, 16, i_count, d_count), BF16)],
        compiler_params=LIMIT,
        name="wide_product",
    )(*on_chip(*parts, *tiles))


def cols_product(parts, tiles, transposed, wire, far):
    i_count, d_count = parts[0].shape[-2:]
    cuts = (tiles[0].shape[0] if transposed else tiles[0].shape[1]) // d_count

    def kernel(*refs):
        ins = refs[:4]
        tile_refs = refs[4:6]
        outs = refs[6:10]
        rows_ref = refs[10]
        z, x, _, y, zh = place()
        for s in range(4):
            ys = (y + 4 - s) % 4
            for q in range(2):
                for half in range(2):
                    xs = (zh ^ q) * 2 + half
                    at = ((xs + 4 - x) % 4) * 4 + (ys ^ z)
                    for k in range(2):
                        rows_ref[k, at] = ins[s][q, k, half]

        @pl.loop(0, cuts)
        def _(n):
            cut = pl.ds(pl.multiple_of(n * d_count, d_count), d_count)
            acc = None
            for k in range(2):
                rows = rows_ref[k].reshape(16 * i_count, d_count)
                part = dot(rows, tile_refs[k][cut, :] if transposed else tile_refs[k][:, cut], transposed)
                acc = part if acc is None else acc + part
            acc = acc.reshape(4, 4, i_count, d_count)
            for s in range(4):
                outs[s][:, n] = acc[s].astype(outs[s].dtype)

    shape = (4, cuts, i_count, d_count)
    return pl.pallas_call(
        kernel,
        out_shape=[sds(shape, (F32, wire, far, wire)[s]) for s in range(4)],
        in_specs=vmem(6),
        out_specs=vmem(4),
        scratch_shapes=[pltpu.VMEM((2, 16, i_count, d_count), BF16)],
        compiler_params=LIMIT,
        name="cols_product",
    )(*on_chip(*parts, *tiles))


def summed(arrays, wire, depth):
    lead = arrays[0].shape[:depth]
    inside = arrays[0].shape[depth:]
    places = [()]
    for size in lead:
        places = [at + (n,) for at in places for n in range(size)]

    def kernel(*refs):
        ins = refs[: len(arrays)]
        outs = refs[len(arrays) :]
        for out, at in zip(outs, places):
            total = ins[0][at].astype(F32)
            for ref in ins[1:]:
                total = total + ref[at].astype(F32)
            out[...] = total.astype(out.dtype)

    return pl.pallas_call(
        kernel,
        out_shape=[sds(inside, F32 if n == 0 else wire) for n in range(len(places))],
        in_specs=vmem(len(arrays)),
        out_specs=vmem(len(places)),
        compiler_params=LIMIT,
        name="summed",
    )(*on_chip(*arrays))


def finished(base, whole, near, far, energies, swap, onward):
    n_base, n_whole, n_near = len(base), len(whole), len(near)
    r_count, i_count, d_count = whole[0].shape

    def kernel(*refs):
        refs = list(refs)

        def take(n):
            taken = refs[:n]
            del refs[:n]
            return taken

        occ_i, occ_j, vir_a, vir_b = take(4)
        bases, wholes, halves = take(n_base), take(n_whole), (take(n_near), take(n_near))
        outs, (stage,) = take(len(shapes)), take(1)
        z, x, core, y, zh = place()
        wide, cols = (z * 4 + x) * 2 + core, y * 2 + zh
        row = lax.broadcasted_iota(jnp.int32, (i_count, d_count), 0)
        occ = jnp.zeros((i_count, d_count), F32)
        for i in range(i_count):
            occ = jnp.where(row == i, occ_i[i], occ)
        for ref in bases:
            for r in range(r_count):
                stage[r] = ref[:, r, :].astype(F32)
        for k in range(2):
            for half in range(2):
                r = half * 2 + (core ^ k)
                total = wholes[0][r].astype(F32)
                for ref in wholes[1:]:
                    total = total + ref[r].astype(F32)
                for ref in halves[k]:
                    total = total + ref[0, half].astype(F32)
                if n_base:
                    total = total + stage[r]
                place_j, place_a = (cols * r_count + r, wide) if swap else (wide, cols * r_count + r)
                total = total / (vir_a[place_a] + vir_b[...] - occ - occ_j[place_j])
                stage[r] = total
                if onward:
                    rounded = total.astype(BF16)
                    outs[1][r] = rounded
                    outs[2 + k][half] = rounded
        for r in range(r_count):
            outs[0][:, r, :] = stage[r]

    shapes = [jax.ShapeDtypeStruct((i_count, r_count, d_count), F32)]
    if onward:
        shapes += [sds((r_count, i_count, d_count), BF16)] + [sds((r_count // 2, i_count, d_count), BF16)] * 2
    return pl.pallas_call(
        kernel,
        out_shape=shapes,
        in_specs=smem(3) + vmem(n_base + n_whole + 2 * n_near + 1),
        out_specs=vmem(len(shapes)),
        scratch_shapes=[pltpu.VMEM((r_count, i_count, d_count), F32)],
        compiler_params=LIMIT,
        name="finished",
    )(*energies[:3], *on_chip(energies[3][None], *base, *whole, *near, *far))


def prepared(amps):
    i_count, r_count, d_count = amps.shape

    def kernel(in_ref, all_ref, near_ref, far_ref):
        core = lax.axis_index("core")
        for r in range(r_count):
            all_ref[r] = in_ref[:, r, :]
        for half in range(r_count // 2):
            near_ref[half] = all_ref[half * 2 + core]
            far_ref[half] = all_ref[half * 2 + (core ^ 1)]

    return pl.pallas_call(
        kernel,
        out_shape=[sds((r_count, i_count, d_count), BF16)] + [sds((r_count // 2, i_count, d_count), BF16)] * 2,
        in_specs=vmem(1),
        out_specs=vmem(3),
        compiler_params=LIMIT,
        name="prepared",
    )(amps)


def wide_gather(piece):
    parts = joined([piece] + [flipped(piece, "sec", m) for m in FLIPS])
    here = {0: parts}
    for s in SHIFTS:
        here[s] = shifted(parts, "rx", s)
    return [here[s] for s in range(4)]


def cols_gather(near, far):
    half = joined([near, swapped(far, ("core",))])
    parts = joined([half, swapped(half, ("zh",))])
    here = {0: parts}
    for s in SHIFTS:
        here[s] = shifted(parts, "y", s)
    return [here[s] for s in range(4)]


def split_sum(arrays):
    inside = (arrays[0].shape[0], *arrays[0].shape[2:])

    def kernel(*refs):
        ins, outs = refs[:-2], refs[-2:]
        for flip in range(inside[0]):
            for q in range(2):
                total = ins[0][flip, q].astype(F32)
                for ref in ins[1:]:
                    total = total + ref[flip, q].astype(F32)
                outs[q][flip] = total.astype(outs[q].dtype)

    return pl.pallas_call(
        kernel,
        out_shape=[sds(inside, F32)] * 2,
        in_specs=vmem(len(arrays)),
        out_specs=vmem(2),
        compiler_params=LIMIT,
        name="split_sum",
    )(*on_chip(*arrays))


def woven(near, far, wire):
    _, count, i_count, n_cols = near.shape

    def kernel(near_ref, far_ref, out_ref):
        core = lax.axis_index("core")
        for half in range(count):
            out_ref[half * 2 + core] = near_ref[1, half].astype(out_ref.dtype)
            out_ref[half * 2 + (core ^ 1)] = far_ref[1, half].astype(out_ref.dtype)

    return pl.pallas_call(
        kernel,
        out_shape=sds((2 * count, i_count, n_cols), wire),
        in_specs=vmem(2),
        out_specs=vmem(1)[0],
        compiler_params=LIMIT,
        name="woven",
    )(*on_chip(near, far))


def cols_sum(outs, wire):
    near, away = split_sum([outs[0]] + [shifted(outs[s], "y", s) for s in SHIFTS])
    far = swapped(away, ("core",))
    return swapped(woven(near, far, wire), ("zh",)), [near], [far]


def wide_sum(outs, wire):
    arrays = [outs[0]] + [shifted(outs[s], "rx", s) for s in SHIFTS]
    parts = summed(arrays, wire, 1)
    return [parts[0]] + [flipped(parts[m], "sec", m) for m in FLIPS]


def sweep(piece, near, far, wide_tiles, cols_tiles, transposed, wire):
    wide_parts = wide_gather(piece)
    cols_parts = cols_gather(near, far)
    outs = cols_product(cols_parts, cols_tiles, transposed, wire, wire)
    whole = wide_sum(outs, wire)
    outs = wide_product(wide_parts, wide_tiles, transposed, wire)
    zh, near, far = cols_sum(outs, wire)
    return whole + [zh], near, far


def body(
    amps,
    driver,
    ladder_operator,
    ladder_block_mask,
    cycle_op,
    cycle_mask,
    occ_i,
    occ_j,
    vir_a,
    vir_b,
):
    energies = (occ_i, occ_j, vir_a, vir_b)
    start = prepared(amps[:, 0])
    cycle_tile = mask_tile(cycle_op, cycle_mask, False)
    ladder_tile = mask_tile(ladder_operator, ladder_block_mask, True)
    cycle_tiles = (cycle_tile, swapped(cycle_tile, ("core",)))
    ladder_tiles = (ladder_tile, swapped(ladder_tile, ("core",)))
    sums = sweep(*start, ladder_tiles, cycle_tiles, False, F32)
    amp_one, *start = finished([driver[:, :, 0]], *sums, energies, True, True)
    sums = sweep(*start, cycle_tiles, ladder_tiles, True, BF16)
    (amp_two,) = finished([], *sums, energies, False, False)
    return amp_one[:, :, None], amp_two[:, None]


def solution(mesh):
    split = Mesh(mesh.devices.reshape(4, 4, 2, 4, 2), AXES)
    return jax.shard_map(
        body,
        mesh=split,
        in_specs=(
            P(None, WIDE, COLS, None),
            P(None, COLS, WIDE, None),
            P(COLS, WIDE),
            P(COLS, WIDE),
            P(WIDE, COLS),
            P(WIDE, COLS),
            P(),
            P(),
            P(),
            P(),
        ),
        out_specs=(P(None, COLS, WIDE, None), P(None, WIDE, COLS, None)),
        check_vma=False,
    )
```
